256 devices in a mesh: occ: 8 (over x_lo, y), vir: 32 (over z, x_hi, core).
Axes of the slice: x: 4 (x_hi: 2, x_lo: 2; x = x_hi * 2 + x_lo), y: 4, z: 8, core: 2. Of those that a mesh axis runs over, the one named last changes fastest.
Arguments:
- amplitudes: bfloat16 [8192, 65536], P('occ', 'vir'), may hold values from -6 to 6
- integrals: bfloat16 [65536, 2048], P('vir', 'occ'), may hold values from -0.125 to 0.125
- ij_irrep: int32 [8192], P('occ'), may hold values from 0 to 7
- cd_irrep: int32 [65536], P('vir'), may hold values from 0 to 7
Outputs:
- ladder: float32 [8192, 2048], P('occ', 'vir')
The draws below stay inside these ranges and needn't reach their ends.
All inputs are finite; a program needn't handle non-finite values.
Results may differ from the reference program's by a relative error of at most 0.0003.
Values may be sent and summed in bfloat16 or wider, within the bound.
A program may use at most 64 MiB of HBM per device.

```python
import jax
import jax.numpy as jnp
from jax import lax

NAB = 2048
NIJ = 8192
NCD = 65536


def with_ends(array, rng, least, top_value):
    shape = array.shape
    spot = [jax.random.randint(jax.random.fold_in(rng, axis), (), 0, shape[axis]) for axis in range(len(shape))]
    array = array.at[tuple(spot)].set(least)
    longest = shape.index(max(shape))
    spot[longest] = (spot[longest] + 1) % shape[longest]
    return array.at[tuple(spot)].set(top_value)


def raised(drawn, rng, source, target, blocks, factor):
    def block_of(axis_at):
        return (jnp.arange(drawn.shape[axis_at]) // (drawn.shape[axis_at] // blocks)).reshape((-1,) + (1,) * (drawn.ndim - 1 - axis_at))

    first = jax.random.permutation(rng, blocks)[block_of(target)]
    other_side = (block_of(target) + blocks // 2) % blocks
    return jnp.where((block_of(source) == first) | (block_of(source) == other_side), factor * drawn, drawn)


def block_scale(own_key, dims, shards, low, top_value):
    def one(dim, parts):
        heights = jax.random.uniform(jax.random.fold_in(jax.random.fold_in(own_key, 6), dim), (parts,), jnp.float32, low / len(shards), top_value / len(shards))
        return jnp.repeat(jnp.exp(heights), dims[dim] // parts).reshape((-1,) + (1,) * (len(dims) - dim - 1))

    level = one(*shards[0])
    for cut in shards[1:]:
        level = level * one(*cut)
    return level


def gaussian(stream_key, extent, scale, most, split=(), held_as=jnp.bfloat16):
    entries = jax.random.normal(stream_key, extent, jnp.float32) * scale
    if len(split) > 0:
        entries = block_scale(stream_key, extent, split, -0.22, 0.18) * entries
    return jnp.clip(entries, min=-most, max=most).astype(held_as)


def heavy_noise(rng, extent, width, most, shards, heavy, kind=jnp.bfloat16):
    values = width * jax.random.normal(rng, extent, jnp.float32)
    if shards:
        values = values * block_scale(rng, extent, shards, -0.22, 0.18)
    return jnp.clip(raised(values, jax.random.fold_in(rng, 3), *heavy), -most, most).astype(kind)


def setup_inputs(seed: int = 0) -> dict:
    seeds = jax.random.split(jax.random.key(seed), 5)
    amplitudes = gaussian(seeds[0], (NIJ, NCD), 1.0, 6.0, ((0, 8), (1, 32)))
    integrals = heavy_noise(seeds[1], (NCD, NAB), (NCD // 8) ** -0.5, 0.125, ((0, 32), (1, 8)), (0, 1, 32, 2.75))
    ij_irrep = with_ends(jax.random.randint(seeds[2], (NIJ,), 0, 8), jax.random.fold_in(seeds[2], 1), 0, 7).astype(jnp.int32)
    cd_irrep = with_ends(jax.random.randint(seeds[3], (NCD,), 0, 8), jax.random.fold_in(seeds[3], 1), 0, 7).astype(jnp.int32)
    return {"amplitudes": amplitudes, "integrals": integrals, "ij_irrep": ij_irrep, "cd_irrep": cd_irrep}


def reference(amplitudes, integrals, ij_irrep, cd_irrep):
    block_rows = min(1024, amplitudes.shape[0])
    blocks = amplitudes.shape[0] // block_rows
    amp_blocks = amplitudes.reshape(blocks, block_rows, amplitudes.shape[1])
    irrep_blocks = ij_irrep.reshape(blocks, block_rows)

    def one_block(pair):
        rows, labels = pair
        masked = jnp.where(labels[:, None] == cd_irrep[None, :], rows, jnp.zeros_like(rows))
        return jnp.dot(masked, integrals, preferred_element_type=jnp.float32)

    result = lax.map(one_block, (amp_blocks, irrep_blocks))
    return result.reshape(amplitudes.shape[0], integrals.shape[1])
```

```python
import functools

import jax
import jax.numpy as jnp
from jax import lax
from jax.experimental import pallas as pl
from jax.experimental.pallas import tpu as pltpu
from jax.sharding import PartitionSpec as P

MESH = pl.DeviceIdType.MESH

SLOT = {(0, 0): 0, (0, 3): 1, (0, 1): 2, (1, 0): 3, (0, 2): 4, (1, 3): 5, (1, 1): 6, (1, 2): 7}
WHERE = {slot: place for place, slot in SLOT.items()}

EVENTS = (
    (0, 0), (0, 1), (0, 2), (0, 3),
    (1, 0), (2, 1), (3, 0),
    (1, 2), (2, 3), (3, 1),
    (1, 1), (2, 0), (3, 2),
    (1, 3), (2, 2), (3, 3),
    (4, 2), (4, 3), (5, 2),
    (5, 0), (6, 1), (6, 3),
    (5, 3), (4, 0), (4, 1),
    (5, 1), (6, 0), (6, 2),
    (7, 0), (7, 1), (7, 2),
    (7, 3),
)
FORWARDS = {
    9: (
        ("up", 1, 2), ("down", 2, 3), ("across", 1, 2),
        ("up", 3, 0), ("down", 3, 1), ("across", 2, 3),
        ("up", 1, 0), ("down", 2, 1),
        ("up", 3, 1), ("down", 3, 0),
    ),
    15: (("across", 1, 3), ("across", 2, 2)),
    17: (("across", 4, 2), ("across", 4, 3)),
    20: (("up", 5, 0), ("down", 6, 1)),
}
FIRST = (
    ("up", 0, 0), ("down", 0, 1), ("across", 0, 0),
    ("up", 0, 2), ("down", 0, 3), ("across", 0, 1),
    ("up", 0, 1), ("down", 0, 0), ("across", 0, 2),
    ("up", 0, 3), ("down", 0, 2), ("across", 0, 3),
)
SENDS = FIRST + tuple(send for event in sorted(FORWARDS) for send in FORWARDS[event])
LAG = 2
TOP = 32767.0


def landing(way, slot):
    other, step = WHERE[slot]
    if way == "up":
        return SLOT[(other, (step - 1) % 4)]
    if way == "down":
        return SLOT[(other, (step + 1) % 4)]
    return SLOT[(1 - other, step)]


def pick(index, values):
    out = jnp.int32(values[-1])
    for at in range(len(values) - 2, -1, -1):
        out = jnp.where(index == at, jnp.int32(values[at]), out)
    return out


def kernel(
    amp_hbm, int_hbm, ij_ref, cd_ref, out_ref,
    amp, blocks, acc, turned, twin, coded, scale, coded_in, scale_in, total, far, ij_col,
    amp_sem, own_sem, send_sem, recv_sem, twin_send, twin_recv,
    z_send, z_recv, s_send, s_recv, far_send, far_recv,
):
    occ, vir = lax.axis_index("occ"), lax.axis_index("vir")
    x_lo, y = occ // 4, occ % 4
    z, x_hi, core = vir // 4, (vir // 2) % 2, vir % 2
    depth = int_hbm.shape[0] // 4

    amp_in = pltpu.make_async_copy(amp_hbm, amp, amp_sem)
    own_in = pltpu.make_async_copy(int_hbm, blocks.at[0], own_sem)
    amp_in.start()
    own_in.start()

    to = {
        "up": (x_lo * 4 + (y + 1) % 4, vir),
        "down": (x_lo * 4 + (y + 3) % 4, vir),
        "across": ((1 - x_lo) * 4 + y, vir),
    }
    sibling = (occ, vir + 1 - 2 * core)
    beyond = (occ, vir + 2 - 4 * x_hi)

    barrier = pltpu.get_barrier_semaphore()
    for device in (to["up"], to["down"], to["across"], sibling, beyond):
        pl.semaphore_signal(barrier, inc=1, device_id=device, device_id_type=MESH)
    for ahead in range(1, 8):
        pl.semaphore_signal(barrier, inc=1, device_id=(occ, (vir + 4 * ahead) % 32), device_id_type=MESH)
    pl.semaphore_wait(barrier, 12)

    def piece(index):
        way, slot, quarter = SENDS[index]
        rows = pl.ds(quarter * depth, depth)
        return pltpu.make_async_remote_copy(
            src_ref=int_hbm.at[rows, :] if slot == 0 else blocks.at[slot, rows, :],
            dst_ref=blocks.at[landing(way, slot), rows, :],
            send_sem=send_sem.at[index],
            recv_sem=recv_sem.at[landing(way, slot), quarter],
            device_id=to[way],
            device_id_type=MESH,
        )

    for index in range(len(FIRST)):
        piece(index).start()

    acc[...] = jnp.zeros_like(acc)
    ij_col[...] = jnp.broadcast_to(ij_ref[...].astype(jnp.float32), (128, ij_ref.shape[1])).T.astype(jnp.bfloat16)
    cd_row = cd_ref[...].astype(jnp.float32).astype(jnp.bfloat16)
    amp_in.wait()
    for at in range(0, amp.shape[1], 128):
        tile = amp[:, at:at + 128]
        amp[:, at:at + 128] = jnp.where(ij_col[...] == cd_row[:, at:at + 128], tile, jnp.zeros_like(tile))
    own_in.wait()

    def owner(slot):
        other = pick(slot, [WHERE[at][0] for at in range(8)])
        step = pick(slot, [WHERE[at][1] for at in range(8)])
        return ((x_lo + other) % 2) * 4 + (y + step) % 4

    def twin_copy(slot):
        return pltpu.make_async_remote_copy(
            src_ref=turned.at[slot, 1 - core],
            dst_ref=twin.at[slot],
            send_sem=twin_send.at[slot],
            recv_sem=twin_recv.at[slot],
            device_id=sibling,
            device_id_type=MESH,
        )

    def z_copies(slot):
        target = owner(slot)
        place = (z - target + 8) % 8
        device = (occ, target * 4 + x_hi * 2 + core)
        return (
            pltpu.make_async_remote_copy(
                src_ref=coded.at[slot], dst_ref=coded_in.at[place],
                send_sem=z_send.at[slot], recv_sem=z_recv.at[place],
                device_id=device, device_id_type=MESH,
            ),
            pltpu.make_async_remote_copy(
                src_ref=scale.at[slot], dst_ref=scale_in.at[place],
                send_sem=s_send.at[slot], recv_sem=s_recv.at[place],
                device_id=device, device_id_type=MESH,
            ),
        )

    last_of = {}
    for event, (slot, _) in enumerate(EVENTS):
        last_of[slot] = event
    ends = [int(last_of[slot] == event) for event, (slot, _) in enumerate(EVENTS)]
    slots = [slot for slot, _ in EVENTS]
    quarters = [quarter for _, quarter in EVENTS]

    @pl.loop(0, len(EVENTS) + LAG)
    def _(event):
        @pl.when(event < len(EVENTS))
        def _():
            slot, quarter = pick(event, slots), pick(event, quarters)
            rows = pl.ds(pl.multiple_of(quarter * depth, depth), depth)

            @pl.when(slot > 0)
            def _():
                pltpu.make_async_remote_copy(
                    src_ref=blocks.at[slot, rows, :], dst_ref=blocks.at[slot, rows, :],
                    send_sem=send_sem.at[0], recv_sem=recv_sem.at[slot, quarter],
                    device_id=to["up"], device_id_type=MESH,
                ).wait_recv()

            index = len(FIRST)
            for after in sorted(FORWARDS):
                @pl.when(event == after)
                def _(index=index, count=len(FORWARDS[after])):
                    for at in range(count):
                        piece(index + at).start()
                index += len(FORWARDS[after])

            acc[slot] += jnp.dot(amp[:, rows], blocks[slot, rows, :], preferred_element_type=jnp.float32)

            @pl.when(pick(event, ends) == 1)
            def _():
                block = acc[slot].T
                for half in range(2):
                    turned[slot, half, 0:64, :] = block[64 * half:64 * half + 64]
                    turned[slot, half, 64:128, :] = block[128 + 64 * half:192 + 64 * half]
                twin_copy(slot).start()

        earlier = jnp.maximum(event - LAG, 0)

        @pl.when((event >= LAG) & (pick(earlier, ends) == 1))
        def _():
            slot = pick(earlier, slots)
            twin_copy(slot).wait_recv()
            both = turned[slot, core] + twin[slot]
            here = owner(slot) == z

            @pl.when(here)
            def _():
                total[...] = both

            @pl.when(jnp.logical_not(here))
            def _():
                most = jnp.maximum(jnp.max(jnp.abs(both), axis=0, keepdims=True), 1e-30)
                scale[slot] = most * (1.0 / TOP)
                coded[slot] = jnp.round(both * (TOP / most)).astype(jnp.int32).astype(jnp.int16)
                for copy in z_copies(slot):
                    copy.start()

    @pl.loop(1, 8)
    def _(place):
        pltpu.make_async_copy(coded_in.at[place], coded_in.at[place], z_recv.at[place]).wait()
        pltpu.make_async_copy(scale_in.at[place], scale_in.at[place], s_recv.at[place]).wait()
        total[...] += coded_in[place].astype(jnp.int32).astype(jnp.float32) * scale_in[place]

    away = pltpu.make_async_remote_copy(
        src_ref=total.at[pl.ds(pl.multiple_of(64 * (1 - x_hi), 64), 64), :],
        dst_ref=far,
        send_sem=far_send, recv_sem=far_recv,
        device_id=beyond, device_id_type=MESH,
    )
    away.start()
    away.wait_recv()
    out_ref[...] = total[pl.ds(pl.multiple_of(64 * x_hi, 64), 64), :] + far[...]

    away.wait_send()
    for index in range(len(SENDS)):
        piece(index).wait_send()

    @pl.loop(0, 8)
    def _(slot):
        twin_copy(slot).wait_send()

        @pl.when(owner(slot) != z)
        def _():
            for copy in z_copies(slot):
                copy.wait_send()


def body(amplitudes, integrals, ij_irrep, cd_irrep):
    rows, deep = amplitudes.shape
    wide = integrals.shape[1]
    any_space = pl.BlockSpec(memory_space=pl.ANY)
    vmem = pl.BlockSpec(memory_space=pltpu.VMEM)
    dma = pltpu.SemaphoreType.DMA
    out = pl.pallas_call(
        kernel,
        out_shape=jax.ShapeDtypeStruct((64, rows), jnp.float32),
        in_specs=[any_space, any_space, vmem, vmem],
        out_specs=vmem,
        scratch_shapes=[
            pltpu.VMEM((rows, deep), jnp.bfloat16),
            pltpu.VMEM((8, deep, wide), jnp.bfloat16),
            pltpu.VMEM((8, rows, wide), jnp.float32),
            pltpu.VMEM((8, 2, 128, rows), jnp.float32),
            pltpu.VMEM((8, 128, rows), jnp.float32),
            pltpu.VMEM((8, 128, rows), jnp.int16),
            pltpu.VMEM((8, 1, rows), jnp.float32),
            pltpu.VMEM((8, 128, rows), jnp.int16),
            pltpu.VMEM((8, 1, rows), jnp.float32),
            pltpu.VMEM((128, rows), jnp.float32),
            pltpu.VMEM((64, rows), jnp.float32),
            pltpu.VMEM((rows, 128), jnp.bfloat16),
            dma, dma, dma((len(SENDS),)), dma((8, 4)), dma((8,)), dma((8,)),
            dma((8,)), dma((8,)), dma((8,)), dma((8,)), dma, dma,
        ],
        compiler_params=pltpu.CompilerParams(
            collective_id=0, has_side_effects=True, vmem_limit_bytes=60 << 20
        ),
        name="ladder",
    )(amplitudes, integrals, ij_irrep.reshape(1, rows), cd_irrep.reshape(1, deep))
    return out.T


def solution(mesh):
    in_specs = (P("occ", "vir"), P("vir", "occ"), P("occ"), P("vir"))
    out_specs = P("occ", "vir")
    return jax.shard_map(body, mesh=mesh, in_specs=in_specs, out_specs=out_specs, check_vma=False)
```

```python
import functools

import jax
import jax.numpy as jnp
from jax import lax
from jax.experimental import pallas as pl
from jax.experimental.pallas import tpu as pltpu
from jax.sharding import PartitionSpec as P

MESH = pl.DeviceIdType.MESH

SLOT = {(0, 0): 0, (0, 3): 1, (0, 1): 2, (1, 0): 3, (0, 2): 4, (1, 3): 5, (1, 1): 6, (1, 2): 7}
WHERE = {slot: place for place, slot in SLOT.items()}

EVENTS = (
    (0, 0), (0, 1), (0, 2), (0, 3),
    (1, 0), (2, 1), (3, 0),
    (1, 2), (2, 3), (3, 1),
    (1, 1), (2, 0), (3, 2),
    (1, 3), (2, 2), (3, 3),
    (4, 2), (4, 3), (5, 2),
    (5, 0), (6, 1), (6, 3),
    (5, 3), (4, 0), (4, 1),
    (5, 1), (6, 0), (6, 2),
    (7, 0), (7, 1), (7, 2),
    (7, 3),
)
FORWARDS = {
    9: (
        ("up", 1, 2), ("down", 2, 3), ("across", 1, 2),
        ("up", 3, 0), ("down", 3, 1), ("across", 2, 3),
        ("up", 1, 0), ("down", 2, 1),
        ("up", 3, 1), ("down", 3, 0),
    ),
    15: (("across", 1, 3), ("across", 2, 2)),
    17: (("across", 4, 2), ("across", 4, 3)),
    20: (("up", 5, 0), ("down", 6, 1)),
}
FIRST = (
    ("up", 0, 0), ("down", 0, 1), ("across", 0, 0),
    ("up", 0, 2), ("down", 0, 3), ("across", 0, 1),
    ("up", 0, 1), ("down", 0, 0), ("across", 0, 2),
    ("up", 0, 3), ("down", 0, 2), ("across", 0, 3),
)
SENDS = FIRST + tuple(send for event in sorted(FORWARDS) for send in FORWARDS[event])
LAG = 2
FOLD = 6
FOLDED = (2, 4, 5)
DIRECT = (7, 1, 6, 3)
TOP = 32767.0


def landing(way, slot):
    other, step = WHERE[slot]
    if way == "up":
        return SLOT[(other, (step - 1) % 4)]
    if way == "down":
        return SLOT[(other, (step + 1) % 4)]
    return SLOT[(1 - other, step)]


def pick(index, values):
    out = jnp.int32(values[-1])
    for at in range(len(values) - 2, -1, -1):
        out = jnp.where(index == at, jnp.int32(values[at]), out)
    return out


def is_in(place, places):
    out = place == places[0]
    for other in places[1:]:
        out = out | (place == other)
    return out


def kernel(
    amp_hbm, int_hbm, ij_ref, cd_ref, out_ref,
    amp, blocks, acc, turned, twin, coded, scale, coded_in, scale_in, total, far, ij_col,
    amp_sem, own_sem, send_sem, recv_sem, twin_send, twin_recv,
    z_send, z_recv, s_send, s_recv, far_send, far_recv,
):
    occ, vir = lax.axis_index("occ"), lax.axis_index("vir")
    x_lo, y = occ // 4, occ % 4
    z, x_hi, core = vir // 4, (vir // 2) % 2, vir % 2
    depth = int_hbm.shape[0] // 4

    amp_in = pltpu.make_async_copy(amp_hbm, amp, amp_sem)
    own_in = pltpu.make_async_copy(int_hbm, blocks.at[0], own_sem)
    amp_in.start()
    own_in.start()

    to = {
        "up": (x_lo * 4 + (y + 1) % 4, vir),
        "down": (x_lo * 4 + (y + 3) % 4, vir),
        "across": ((1 - x_lo) * 4 + y, vir),
    }
    sibling = (occ, vir + 1 - 2 * core)
    beyond = (occ, vir + 2 - 4 * x_hi)

    barrier = pltpu.get_barrier_semaphore()
    for device in (to["up"], to["down"], to["across"], sibling, beyond):
        pl.semaphore_signal(barrier, inc=1, device_id=device, device_id_type=MESH)
    for ahead in range(1, 8):
        pl.semaphore_signal(barrier, inc=1, device_id=(occ, (vir + 4 * ahead) % 32), device_id_type=MESH)
    pl.semaphore_wait(barrier, 12)

    def piece(index):
        way, slot, quarter = SENDS[index]
        rows = pl.ds(quarter * depth, depth)
        return pltpu.make_async_remote_copy(
            src_ref=int_hbm.at[rows, :] if slot == 0 else blocks.at[slot, rows, :],
            dst_ref=blocks.at[landing(way, slot), rows, :],
            send_sem=send_sem.at[index],
            recv_sem=recv_sem.at[landing(way, slot), quarter],
            device_id=to[way],
            device_id_type=MESH,
        )

    for index in range(len(FIRST)):
        piece(index).start()

    acc[...] = jnp.zeros_like(acc)
    ij_col[...] = jnp.broadcast_to(ij_ref[...].astype(jnp.float32), (128, ij_ref.shape[1])).T.astype(jnp.bfloat16)
    cd_row = cd_ref[...].astype(jnp.float32).astype(jnp.bfloat16)
    amp_in.wait()
    for at in range(0, amp.shape[1], 128):
        tile = amp[:, at:at + 128]
        amp[:, at:at + 128] = jnp.where(ij_col[...] == cd_row[:, at:at + 128], tile, jnp.zeros_like(tile))
    own_in.wait()

    def owner(slot):
        other = pick(slot, [WHERE[at][0] for at in range(8)])
        step = pick(slot, [WHERE[at][1] for at in range(8)])
        return ((x_lo + other) % 2) * 4 + (y + step) % 4

    def twin_copy(slot):
        return pltpu.make_async_remote_copy(
            src_ref=turned.at[slot, 1 - core],
            dst_ref=twin.at[slot],
            send_sem=twin_send.at[slot],
            recv_sem=twin_recv.at[slot],
            device_id=sibling,
            device_id_type=MESH,
        )

    def z_copies(slot):
        target = owner(slot)
        place = (z - target + 8) % 8
        folded = is_in(place, FOLDED)
        nearer = jnp.where(place == 5, (z + 1) % 8, (z + 7) % 8)
        place = jnp.where(folded, 8 + slot, place)
        device = (occ, jnp.where(folded, nearer, target) * 4 + x_hi * 2 + core)
        return (
            pltpu.make_async_remote_copy(
                src_ref=coded.at[slot], dst_ref=coded_in.at[place],
                send_sem=z_send.at[slot], recv_sem=z_recv.at[place],
                device_id=device, device_id_type=MESH,
            ),
            pltpu.make_async_remote_copy(
                src_ref=scale.at[slot], dst_ref=scale_in.at[place],
                send_sem=s_send.at[slot], recv_sem=s_recv.at[place],
                device_id=device, device_id_type=MESH,
            ),
        )

    last_of = {}
    for event, (slot, _) in enumerate(EVENTS):
        last_of[slot] = event
    ends = [int(last_of[slot] == event) for event, (slot, _) in enumerate(EVENTS)]
    slots = [slot for slot, _ in EVENTS]
    quarters = [quarter for _, quarter in EVENTS]

    def send(slot, both):
        most = jnp.maximum(jnp.max(jnp.abs(both), axis=0, keepdims=True), 1e-30)
        scale[slot] = most * (1.0 / TOP)
        coded[slot] = jnp.round(both * (TOP / most)).astype(jnp.int32).astype(jnp.int16)
        for copy in z_copies(slot):
            copy.start()

    def arrived(place):
        pltpu.make_async_copy(coded_in.at[place], coded_in.at[place], z_recv.at[place]).wait()
        pltpu.make_async_copy(scale_in.at[place], scale_in.at[place], s_recv.at[place]).wait()
        return coded_in[place].astype(jnp.int32).astype(jnp.float32) * scale_in[place]

    @pl.loop(0, len(EVENTS) + LAG + FOLD)
    def _(event):
        @pl.when(event < len(EVENTS))
        def _():
            slot, quarter = pick(event, slots), pick(event, quarters)
            rows = pl.ds(pl.multiple_of(quarter * depth, depth), depth)

            @pl.when(slot > 0)
            def _():
                pltpu.make_async_remote_copy(
                    src_ref=blocks.at[slot, rows, :], dst_ref=blocks.at[slot, rows, :],
                    send_sem=send_sem.at[0], recv_sem=recv_sem.at[slot, quarter],
                    device_id=to["up"], device_id_type=MESH,
                ).wait_recv()

            index = len(FIRST)
            for after in sorted(FORWARDS):
                @pl.when(event == after)
                def _(index=index, count=len(FORWARDS[after])):
                    for at in range(count):
                        piece(index + at).start()
                index += len(FORWARDS[after])

            acc[slot] += jnp.dot(amp[:, rows], blocks[slot, rows, :], preferred_element_type=jnp.float32)

            @pl.when(pick(event, ends) == 1)
            def _():
                block = acc[slot].T
                for half in range(2):
                    turned[slot, half, 0:64, :] = block[64 * half:64 * half + 64]
                    turned[slot, half, 64:128, :] = block[128 + 64 * half:192 + 64 * half]
                twin_copy(slot).start()

        earlier = jnp.maximum(event - LAG, 0)

        @pl.when((event >= LAG) & (event < len(EVENTS) + LAG) & (pick(earlier, ends) == 1))
        def _():
            slot = pick(earlier, slots)
            twin_copy(slot).wait_recv()
            both = turned[slot, core] + twin[slot]
            place = (z - owner(slot) + 8) % 8
            adds = is_in(place, (1, 3, 6))

            @pl.when(place == 0)
            def _():
                total[...] = both

            @pl.when(adds)
            def _():
                twin[slot] = both

            @pl.when((place != 0) & jnp.logical_not(adds))
            def _():
                send(slot, both)

        before = jnp.maximum(event - LAG - FOLD, 0)

        @pl.when((event >= LAG + FOLD) & (pick(before, ends) == 1))
        def _():
            slot = pick(before, slots)

            @pl.when(is_in((z - owner(slot) + 8) % 8, (1, 3, 6)))
            def _():
                send(slot, twin[slot] + arrived(8 + slot))

    @pl.loop(0, len(DIRECT))
    def _(at):
        total[...] += arrived(pick(at, DIRECT))

    away = pltpu.make_async_remote_copy(
        src_ref=total.at[pl.ds(pl.multiple_of(64 * (1 - x_hi), 64), 64), :],
        dst_ref=far,
        send_sem=far_send, recv_sem=far_recv,
        device_id=beyond, device_id_type=MESH,
    )
    away.start()
    away.wait_recv()
    out_ref[...] = total[pl.ds(pl.multiple_of(64 * x_hi, 64), 64), :] + far[...]

    away.wait_send()
    for index in range(len(SENDS)):
        piece(index).wait_send()

    @pl.loop(0, 8)
    def _(slot):
        twin_copy(slot).wait_send()

        @pl.when(owner(slot) != z)
        def _():
            for copy in z_copies(slot):
                copy.wait_send()


def body(amplitudes, integrals, ij_irrep, cd_irrep):
    rows, deep = amplitudes.shape
    wide = integrals.shape[1]
    any_space = pl.BlockSpec(memory_space=pl.ANY)
    vmem = pl.BlockSpec(memory_space=pltpu.VMEM)
    dma = pltpu.SemaphoreType.DMA
    out = pl.pallas_call(
        kernel,
        out_shape=jax.ShapeDtypeStruct((64, rows), jnp.float32),
        in_specs=[any_space, any_space, vmem, vmem],
        out_specs=vmem,
        scratch_shapes=[
            pltpu.VMEM((rows, deep), jnp.bfloat16),
            pltpu.VMEM((8, deep, wide), jnp.bfloat16),
            pltpu.VMEM((8, rows, wide), jnp.float32),
            pltpu.VMEM((8, 2, 128, rows), jnp.float32),
            pltpu.VMEM((8, 128, rows), jnp.float32),
            pltpu.VMEM((8, 128, rows), jnp.int16),
            pltpu.VMEM((8, 1, rows), jnp.float32),
            pltpu.VMEM((16, 128, rows), jnp.int16),
            pltpu.VMEM((16, 1, rows), jnp.float32),
            pltpu.VMEM((128, rows), jnp.float32),
            pltpu.VMEM((64, rows), jnp.float32),
            pltpu.VMEM((rows, 128), jnp.bfloat16),
            dma, dma, dma((len(SENDS),)), dma((8, 4)), dma((8,)), dma((8,)),
            dma((8,)), dma((16,)), dma((8,)), dma((16,)), dma, dma,
        ],
        compiler_params=pltpu.CompilerParams(
            collective_id=0, has_side_effects=True, vmem_limit_bytes=60 << 20
        ),
        name="ladder",
    )(amplitudes, integrals, ij_irrep.reshape(1, rows), cd_irrep.reshape(1, deep))
    return out.T


def solution(mesh):
    in_specs = (P("occ", "vir"), P("vir", "occ"), P("occ"), P("vir"))
    out_specs = P("occ", "vir")
    return jax.shard_map(body, mesh=mesh, in_specs=in_specs, out_specs=out_specs, check_vma=False)
```

```python
import functools

import jax
import jax.numpy as jnp
from jax import lax
from jax.experimental import pallas as pl
from jax.experimental.pallas import tpu as pltpu
from jax.sharding import PartitionSpec as P

MESH = pl.DeviceIdType.MESH

SLOT = {(0, 0): 0, (0, 3): 1, (0, 1): 2, (1, 0): 3, (0, 2): 4, (1, 3): 5, (1, 1): 6, (1, 2): 7}
WHERE = {slot: place for place, slot in SLOT.items()}

EVENTS = (
    (0, 0), (0, 1), (0, 2), (0, 3),
    (1, 0), (2, 1), (3, 0),
    (1, 2), (2, 3), (3, 1),
    (1, 1), (2, 0), (3, 2),
    (1, 3), (2, 2), (3, 3),
    (4, 2), (4, 3), (5, 2),
    (5, 0), (6, 1), (6, 3),
    (5, 3), (4, 0), (4, 1),
    (5, 1), (6, 0), (6, 2),
    (7, 0), (7, 1), (7, 2),
    (7, 3),
)
FORWARDS = {
    9: (
        ("up", 1, 2), ("down", 2, 3), ("across", 1, 2),
        ("up", 3, 0), ("down", 3, 1), ("across", 2, 3),
        ("up", 1, 0), ("down", 2, 1),
        ("up", 3, 1), ("down", 3, 0),
    ),
    15: (("across", 1, 3), ("across", 2, 2)),
    17: (("across", 4, 2), ("across", 4, 3)),
    20: (("up", 5, 0), ("down", 6, 1)),
}
FIRST = (
    ("up", 0, 0), ("down", 0, 1), ("across", 0, 0),
    ("up", 0, 2), ("down", 0, 3), ("across", 0, 1),
    ("up", 0, 1), ("down", 0, 0), ("across", 0, 2),
    ("up", 0, 3), ("down", 0, 2), ("across", 0, 3),
)
SENDS = FIRST + tuple(send for event in sorted(FORWARDS) for send in FORWARDS[event])
LAG = 2
FOLD = 6
PARTS = 4
FOLDED = (2, 4, 5)
DIRECT = (7, 1, 6, 3)
TOP = 32767.0


def landing(way, slot):
    other, step = WHERE[slot]
    if way == "up":
        return SLOT[(other, (step - 1) % 4)]
    if way == "down":
        return SLOT[(other, (step + 1) % 4)]
    return SLOT[(1 - other, step)]


def pick(index, values):
    out = jnp.int32(values[-1])
    for at in range(len(values) - 2, -1, -1):
        out = jnp.where(index == at, jnp.int32(values[at]), out)
    return out


def is_in(place, places):
    out = place == places[0]
    for other in places[1:]:
        out = out | (place == other)
    return out


def kernel(
    amp_hbm, int_hbm, ij_ref, cd_ref, out_ref,
    amp, blocks, acc, turned, twin, coded, scale, coded_in, scale_in, total, far, ij_col,
    amp_sem, own_sem, send_sem, recv_sem, twin_send, twin_recv,
    z_send, z_recv, s_send, s_recv, far_send, far_recv,
):
    occ, vir = lax.axis_index("occ"), lax.axis_index("vir")
    x_lo, y = occ // 4, occ % 4
    z, x_hi, core = vir // 4, (vir // 2) % 2, vir % 2
    depth = int_hbm.shape[0] // 4
    wide = amp_hbm.shape[0] // PARTS

    amp_in = pltpu.make_async_copy(amp_hbm, amp, amp_sem)
    own_in = pltpu.make_async_copy(int_hbm, blocks.at[0], own_sem)
    amp_in.start()
    own_in.start()

    to = {
        "up": (x_lo * 4 + (y + 1) % 4, vir),
        "down": (x_lo * 4 + (y + 3) % 4, vir),
        "across": ((1 - x_lo) * 4 + y, vir),
    }
    sibling = (occ, vir + 1 - 2 * core)
    beyond = (occ, vir + 2 - 4 * x_hi)

    barrier = pltpu.get_barrier_semaphore()
    for device in (to["up"], to["down"], to["across"], sibling, beyond):
        pl.semaphore_signal(barrier, inc=1, device_id=device, device_id_type=MESH)
    for ahead in range(1, 8):
        pl.semaphore_signal(barrier, inc=1, device_id=(occ, (vir + 4 * ahead) % 32), device_id_type=MESH)
    pl.semaphore_wait(barrier, 12)

    def piece(index):
        way, slot, quarter = SENDS[index]
        rows = pl.ds(quarter * depth, depth)
        return pltpu.make_async_remote_copy(
            src_ref=int_hbm.at[rows, :] if slot == 0 else blocks.at[slot, rows, :],
            dst_ref=blocks.at[landing(way, slot), rows, :],
            send_sem=send_sem.at[index],
            recv_sem=recv_sem.at[landing(way, slot), quarter],
            device_id=to[way],
            device_id_type=MESH,
        )

    for index in range(len(FIRST)):
        piece(index).start()

    acc[...] = jnp.zeros_like(acc)
    ij_col[...] = jnp.broadcast_to(ij_ref[...].astype(jnp.float32), (128, ij_ref.shape[1])).T.astype(jnp.bfloat16)
    cd_row = cd_ref[...].astype(jnp.float32).astype(jnp.bfloat16)
    amp_in.wait()
    for at in range(0, amp.shape[1], 128):
        tile = amp[:, at:at + 128]
        amp[:, at:at + 128] = jnp.where(ij_col[...] == cd_row[:, at:at + 128], tile, jnp.zeros_like(tile))
    own_in.wait()

    def owner(slot):
        other = pick(slot, [WHERE[at][0] for at in range(8)])
        step = pick(slot, [WHERE[at][1] for at in range(8)])
        return ((x_lo + other) % 2) * 4 + (y + step) % 4

    def twin_copy(slot):
        return pltpu.make_async_remote_copy(
            src_ref=turned.at[slot, 1 - core],
            dst_ref=twin.at[slot],
            send_sem=twin_send.at[slot],
            recv_sem=twin_recv.at[slot],
            device_id=sibling,
            device_id_type=MESH,
        )

    def z_copies(slot, part):
        target = owner(slot)
        place = (z - target + 8) % 8
        folded = is_in(place, FOLDED)
        nearer = jnp.where(place == 5, (z + 1) % 8, (z + 7) % 8)
        place = jnp.where(folded, 8 + slot, place)
        device = (occ, jnp.where(folded, nearer, target) * 4 + x_hi * 2 + core)
        return (
            pltpu.make_async_remote_copy(
                src_ref=coded.at[slot, part], dst_ref=coded_in.at[place, part],
                send_sem=z_send.at[slot, part], recv_sem=z_recv.at[place, part],
                device_id=device, device_id_type=MESH,
            ),
            pltpu.make_async_remote_copy(
                src_ref=scale.at[slot, part], dst_ref=scale_in.at[place, part],
                send_sem=s_send.at[slot, part], recv_sem=s_recv.at[place, part],
                device_id=device, device_id_type=MESH,
            ),
        )

    last_of = {}
    for event, (slot, _) in enumerate(EVENTS):
        last_of[slot] = event
    ends = [int(last_of[slot] == event) for event, (slot, _) in enumerate(EVENTS)]
    slots = [slot for slot, _ in EVENTS]
    quarters = [quarter for _, quarter in EVENTS]

    def send(slot, part, both):
        most = jnp.maximum(jnp.max(jnp.abs(both), axis=0, keepdims=True), 1e-30)
        scale[slot, part] = most * (1.0 / TOP)
        coded[slot, part] = jnp.round(both * (TOP / most)).astype(jnp.int32).astype(jnp.int16)
        for copy in z_copies(slot, part):
            copy.start()

    def arrived(place, part):
        code, step = coded_in.at[place, part], scale_in.at[place, part]
        pltpu.make_async_copy(code, code, z_recv.at[place, part]).wait()
        pltpu.make_async_copy(step, step, s_recv.at[place, part]).wait()
        return coded_in[place, part].astype(jnp.int32).astype(jnp.float32) * scale_in[place, part]

    def columns(part):
        return slice(part * wide, (part + 1) * wide)

    @pl.loop(0, len(EVENTS) + LAG + FOLD)
    def _(event):
        @pl.when(event < len(EVENTS))
        def _():
            slot, quarter = pick(event, slots), pick(event, quarters)
            rows = pl.ds(pl.multiple_of(quarter * depth, depth), depth)

            @pl.when(slot > 0)
            def _():
                pltpu.make_async_remote_copy(
                    src_ref=blocks.at[slot, rows, :], dst_ref=blocks.at[slot, rows, :],
                    send_sem=send_sem.at[0], recv_sem=recv_sem.at[slot, quarter],
                    device_id=to["up"], device_id_type=MESH,
                ).wait_recv()

            index = len(FIRST)
            for after in sorted(FORWARDS):
                @pl.when(event == after)
                def _(index=index, count=len(FORWARDS[after])):
                    for at in range(count):
                        piece(index + at).start()
                index += len(FORWARDS[after])

            acc[slot] += jnp.dot(amp[:, rows], blocks[slot, rows, :], preferred_element_type=jnp.float32)

            @pl.when(pick(event, ends) == 1)
            def _():
                block = acc[slot].T
                for half in range(2):
                    turned[slot, half, 0:64, :] = block[64 * half:64 * half + 64]
                    turned[slot, half, 64:128, :] = block[128 + 64 * half:192 + 64 * half]
                twin_copy(slot).start()

        earlier = jnp.maximum(event - LAG, 0)

        @pl.when((event >= LAG) & (event < len(EVENTS) + LAG) & (pick(earlier, ends) == 1))
        def _():
            slot = pick(earlier, slots)
            twin_copy(slot).wait_recv()
            place = (z - owner(slot) + 8) % 8
            adds = is_in(place, (1, 3, 6))

            @pl.when(place == 0)
            def _():
                for part in range(PARTS):
                    total[part] = turned[slot, core, :, columns(part)] + twin[slot, :, columns(part)]

            @pl.when(adds)
            def _():
                twin[slot] = turned[slot, core] + twin[slot]

            @pl.when((place != 0) & jnp.logical_not(adds))
            def _():
                for part in range(PARTS):
                    send(slot, part, turned[slot, core, :, columns(part)] + twin[slot, :, columns(part)])

        before = jnp.maximum(event - LAG - FOLD, 0)

        @pl.when((event >= LAG + FOLD) & (pick(before, ends) == 1))
        def _():
            slot = pick(before, slots)

            @pl.when(is_in((z - owner(slot) + 8) % 8, (1, 3, 6)))
            def _():
                for part in range(PARTS):
                    send(slot, part, twin[slot, :, columns(part)] + arrived(8 + slot, part))

    def away(part):
        return pltpu.make_async_remote_copy(
            src_ref=total.at[part, pl.ds(pl.multiple_of(64 * (1 - x_hi), 64), 64), :],
            dst_ref=far.at[part],
            send_sem=far_send.at[part], recv_sem=far_recv.at[part],
            device_id=beyond, device_id_type=MESH,
        )

    for part in range(PARTS):
        @pl.loop(0, len(DIRECT))
        def _(at, part=part):
            total[part] += arrived(pick(at, DIRECT), part)

        away(part).start()

    for part in range(PARTS):
        away(part).wait_recv()
        out_ref[:, columns(part)] = total[part, pl.ds(pl.multiple_of(64 * x_hi, 64), 64), :] + far[part]

    for part in range(PARTS):
        away(part).wait_send()
    for index in range(len(SENDS)):
        piece(index).wait_send()

    @pl.loop(0, 8)
    def _(slot):
        twin_copy(slot).wait_send()

        @pl.when(owner(slot) != z)
        def _():
            for part in range(PARTS):
                for copy in z_copies(slot, part):
                    copy.wait_send()


def body(amplitudes, integrals, ij_irrep, cd_irrep):
    rows, deep = amplitudes.shape
    wide = integrals.shape[1]
    any_space = pl.BlockSpec(memory_space=pl.ANY)
    vmem = pl.BlockSpec(memory_space=pltpu.VMEM)
    dma = pltpu.SemaphoreType.DMA
    out = pl.pallas_call(
        kernel,
        out_shape=jax.ShapeDtypeStruct((64, rows), jnp.float32),
        in_specs=[any_space, any_space, vmem, vmem],
        out_specs=vmem,
        scratch_shapes=[
            pltpu.VMEM((rows, deep), jnp.bfloat16),
            pltpu.VMEM((8, deep, wide), jnp.bfloat16),
            pltpu.VMEM((8, rows, wide), jnp.float32),
            pltpu.VMEM((8, 2, 128, rows), jnp.float32),
            pltpu.VMEM((8, 128, rows), jnp.float32),
            pltpu.VMEM((8, PARTS, 128, rows // PARTS), jnp.int16),
            pltpu.VMEM((8, PARTS, 1, rows // PARTS), jnp.float32),
            pltpu.VMEM((16, PARTS, 128, rows // PARTS), jnp.int16),
            pltpu.VMEM((16, PARTS, 1, rows // PARTS), jnp.float32),
            pltpu.VMEM((PARTS, 128, rows // PARTS), jnp.float32),
            pltpu.VMEM((PARTS, 64, rows // PARTS), jnp.float32),
            pltpu.VMEM((rows, 128), jnp.bfloat16),
            dma, dma, dma((len(SENDS),)), dma((8, 4)), dma((8,)), dma((8,)),
            dma((8, PARTS)), dma((16, PARTS)), dma((8, PARTS)), dma((16, PARTS)), dma((PARTS,)), dma((PARTS,)),
        ],
        compiler_params=pltpu.CompilerParams(
            collective_id=0, has_side_effects=True, vmem_limit_bytes=60 << 20
        ),
        name="ladder",
    )(amplitudes, integrals, ij_irrep.reshape(1, rows), cd_irrep.reshape(1, deep))
    return out.T


def solution(mesh):
    in_specs = (P("occ", "vir"), P("vir", "occ"), P("occ"), P("vir"))
    out_specs = P("occ", "vir")
    return jax.shard_map(body, mesh=mesh, in_specs=in_specs, out_specs=out_specs, check_vma=False)
```

```python
import functools

import jax
import jax.numpy as jnp
from jax import lax
from jax.experimental import pallas as pl
from jax.experimental.pallas import tpu as pltpu
from jax.sharding import PartitionSpec as P

MESH = pl.DeviceIdType.MESH

SLOT = {(0, 0): 0, (0, 3): 1, (0, 1): 2, (1, 0): 3, (0, 2): 4, (1, 3): 5, (1, 1): 6, (1, 2): 7}
WHERE = {slot: place for place, slot in SLOT.items()}

EVENTS = (
    (0, 0), (0, 1), (0, 2), (0, 3),
    (1, 0), (2, 1), (3, 0),
    (1, 2), (2, 3), (3, 1),
    (1, 1), (2, 0), (3, 2),
    (1, 3), (2, 2), (3, 3),
    (4, 2), (4, 3), (5, 2),
    (5, 0), (6, 1), (6, 3),
    (5, 3), (4, 0), (4, 1),
    (5, 1), (6, 0), (6, 2),
    (7, 0), (7, 1), (7, 2),
    (7, 3),
)
FORWARDS = {
    9: (
        ("up", 1, 2), ("down", 2, 3), ("across", 1, 2),
        ("up", 3, 0), ("down", 3, 1), ("across", 2, 3),
        ("up", 1, 0), ("down", 2, 1),
        ("up", 3, 1), ("down", 3, 0),
    ),
    15: (("across", 1, 3), ("across", 2, 2)),
    17: (("across", 4, 2), ("across", 4, 3)),
    20: (("up", 5, 0), ("down", 6, 1)),
}
FIRST = (
    ("up", 0, 0), ("down", 0, 1), ("across", 0, 0),
    ("up", 0, 2), ("down", 0, 3), ("across", 0, 1),
    ("up", 0, 1), ("down", 0, 0), ("across", 0, 2),
    ("up", 0, 3), ("down", 0, 2), ("across", 0, 3),
)
SENDS = FIRST + tuple(send for event in sorted(FORWARDS) for send in FORWARDS[event])
LAG = 1
FOLD = 8
PARTS = 4
FOLDED = (2, 4, 5)
DIRECT = (7, 1, 6, 3)
TOP = 32767.0


def landing(way, slot):
    other, step = WHERE[slot]
    if way == "up":
        return SLOT[(other, (step - 1) % 4)]
    if way == "down":
        return SLOT[(other, (step + 1) % 4)]
    return SLOT[(1 - other, step)]


def pick(index, values):
    out = jnp.int32(values[-1])
    for at in range(len(values) - 2, -1, -1):
        out = jnp.where(index == at, jnp.int32(values[at]), out)
    return out


def is_in(place, places):
    out = place == places[0]
    for other in places[1:]:
        out = out | (place == other)
    return out


def kernel(
    amp_hbm, int_hbm, ij_ref, cd_ref, out_ref,
    amp, blocks, acc, turned, twin, coded, scale, coded_in, scale_in, total, far, ij_col,
    amp_sem, own_sem, send_sem, recv_sem, twin_send, twin_recv,
    z_send, z_recv, s_send, s_recv, far_send, far_recv,
):
    occ, vir = lax.axis_index("occ"), lax.axis_index("vir")
    x_lo, y = occ // 4, occ % 4
    z, x_hi, core = vir // 4, (vir // 2) % 2, vir % 2
    depth = int_hbm.shape[0] // 4
    wide = amp_hbm.shape[0] // PARTS

    amp_in = pltpu.make_async_copy(amp_hbm, amp, amp_sem)
    own_in = pltpu.make_async_copy(int_hbm, blocks.at[0], own_sem)
    amp_in.start()
    own_in.start()

    to = {
        "up": (x_lo * 4 + (y + 1) % 4, vir),
        "down": (x_lo * 4 + (y + 3) % 4, vir),
        "across": ((1 - x_lo) * 4 + y, vir),
    }
    sibling = (occ, vir + 1 - 2 * core)
    beyond = (occ, vir + 2 - 4 * x_hi)

    barrier = pltpu.get_barrier_semaphore()
    for device in (to["up"], to["down"], to["across"], sibling, beyond):
        pl.semaphore_signal(barrier, inc=1, device_id=device, device_id_type=MESH)
    for ahead in range(1, 8):
        pl.semaphore_signal(barrier, inc=1, device_id=(occ, (vir + 4 * ahead) % 32), device_id_type=MESH)
    pl.semaphore_wait(barrier, 12)

    def piece(index):
        way, slot, quarter = SENDS[index]
        rows = pl.ds(quarter * depth, depth)
        return pltpu.make_async_remote_copy(
            src_ref=int_hbm.at[rows, :] if slot == 0 else blocks.at[slot, rows, :],
            dst_ref=blocks.at[landing(way, slot), rows, :],
            send_sem=send_sem.at[index],
            recv_sem=recv_sem.at[landing(way, slot), quarter],
            device_id=to[way],
            device_id_type=MESH,
        )

    for index in range(len(FIRST)):
        piece(index).start()

    acc[...] = jnp.zeros_like(acc)
    ij_col[...] = jnp.broadcast_to(ij_ref[...].astype(jnp.float32), (128, ij_ref.shape[1])).T.astype(jnp.bfloat16)
    cd_row = cd_ref[...].astype(jnp.float32).astype(jnp.bfloat16)
    amp_in.wait()
    for at in range(0, amp.shape[1], 128):
        tile = amp[:, at:at + 128]
        amp[:, at:at + 128] = jnp.where(ij_col[...] == cd_row[:, at:at + 128], tile, jnp.zeros_like(tile))
    own_in.wait()

    def owner(slot):
        other = pick(slot, [WHERE[at][0] for at in range(8)])
        step = pick(slot, [WHERE[at][1] for at in range(8)])
        return ((x_lo + other) % 2) * 4 + (y + step) % 4

    def columns(part):
        return slice(part * wide, (part + 1) * wide)

    def twin_copy(slot, part):
        return pltpu.make_async_remote_copy(
            src_ref=turned.at[slot, 1 - core, :, columns(part)],
            dst_ref=twin.at[slot, :, columns(part)],
            send_sem=twin_send.at[slot, part],
            recv_sem=twin_recv.at[slot, part],
            device_id=sibling,
            device_id_type=MESH,
        )

    def z_copies(slot, part):
        target = owner(slot)
        place = (z - target + 8) % 8
        folded = is_in(place, FOLDED)
        nearer = jnp.where(place == 5, (z + 1) % 8, (z + 7) % 8)
        place = jnp.where(folded, 8 + slot, place)
        device = (occ, jnp.where(folded, nearer, target) * 4 + x_hi * 2 + core)
        return (
            pltpu.make_async_remote_copy(
                src_ref=coded.at[slot, part], dst_ref=coded_in.at[place, part],
                send_sem=z_send.at[slot, part], recv_sem=z_recv.at[place, part],
                device_id=device, device_id_type=MESH,
            ),
            pltpu.make_async_remote_copy(
                src_ref=scale.at[slot, part], dst_ref=scale_in.at[place, part],
                send_sem=s_send.at[slot, part], recv_sem=s_recv.at[place, part],
                device_id=device, device_id_type=MESH,
            ),
        )

    last_of = {}
    for event, (slot, _) in enumerate(EVENTS):
        last_of[slot] = event
    ends = [int(last_of[slot] == event) for event, (slot, _) in enumerate(EVENTS)]
    slots = [slot for slot, _ in EVENTS]
    quarters = [quarter for _, quarter in EVENTS]

    def send(slot, part, both):
        most = jnp.maximum(jnp.max(jnp.abs(both), axis=0, keepdims=True), 1e-30)
        scale[slot, part] = most * (1.0 / TOP)
        coded[slot, part] = jnp.round(both * (TOP / most)).astype(jnp.int32).astype(jnp.int16)
        for copy in z_copies(slot, part):
            copy.start()

    def arrived(place, part):
        code, step = coded_in.at[place, part], scale_in.at[place, part]
        pltpu.make_async_copy(code, code, z_recv.at[place, part]).wait()
        pltpu.make_async_copy(step, step, s_recv.at[place, part]).wait()
        return coded_in[place, part].astype(jnp.int32).astype(jnp.float32) * scale_in[place, part]

    def both(slot, part):
        twin_copy(slot, part).wait_recv()
        return turned[slot, core, :, columns(part)] + twin[slot, :, columns(part)]

    @pl.loop(0, len(EVENTS) + LAG + FOLD)
    def _(event):
        @pl.when(event < len(EVENTS))
        def _():
            slot, quarter = pick(event, slots), pick(event, quarters)
            rows = pl.ds(pl.multiple_of(quarter * depth, depth), depth)

            @pl.when(slot > 0)
            def _():
                pltpu.make_async_remote_copy(
                    src_ref=blocks.at[slot, rows, :], dst_ref=blocks.at[slot, rows, :],
                    send_sem=send_sem.at[0], recv_sem=recv_sem.at[slot, quarter],
                    device_id=to["up"], device_id_type=MESH,
                ).wait_recv()

            index = len(FIRST)
            for after in sorted(FORWARDS):
                @pl.when(event == after)
                def _(index=index, count=len(FORWARDS[after])):
                    for at in range(count):
                        piece(index + at).start()
                index += len(FORWARDS[after])

            acc[slot] += jnp.dot(amp[:, rows], blocks[slot, rows, :], preferred_element_type=jnp.float32)

            @pl.when(pick(event, ends) == 1)
            def _():
                for part in range(PARTS):
                    block = acc[slot, columns(part), :].T
                    for half in range(2):
                        turned[slot, half, 0:64, columns(part)] = block[64 * half:64 * half + 64]
                        turned[slot, half, 64:128, columns(part)] = block[128 + 64 * half:192 + 64 * half]
                    twin_copy(slot, part).start()

        earlier = jnp.maximum(event - LAG, 0)

        @pl.when((event >= LAG) & (event < len(EVENTS) + LAG) & (pick(earlier, ends) == 1))
        def _():
            slot = pick(earlier, slots)
            place = (z - owner(slot) + 8) % 8
            adds = is_in(place, (1, 3, 6))

            @pl.when(place == 0)
            def _():
                for part in range(PARTS):
                    total[part] = both(slot, part)

            @pl.when(adds)
            def _():
                for part in range(PARTS):
                    twin[slot, :, columns(part)] = both(slot, part)

            @pl.when((place != 0) & jnp.logical_not(adds))
            def _():
                for part in range(PARTS):
                    send(slot, part, both(slot, part))

        before = jnp.maximum(event - LAG - FOLD, 0)

        @pl.when((event >= LAG + FOLD) & (pick(before, ends) == 1))
        def _():
            slot = pick(before, slots)

            @pl.when(is_in((z - owner(slot) + 8) % 8, (1, 3, 6)))
            def _():
                for part in range(PARTS):
                    send(slot, part, twin[slot, :, columns(part)] + arrived(8 + slot, part))

    def away(part):
        return pltpu.make_async_remote_copy(
            src_ref=total.at[part, pl.ds(pl.multiple_of(64 * (1 - x_hi), 64), 64), :],
            dst_ref=far.at[part],
            send_sem=far_send.at[part], recv_sem=far_recv.at[part],
            device_id=beyond, device_id_type=MESH,
        )

    for part in range(PARTS):
        @pl.loop(0, len(DIRECT))
        def _(at, part=part):
            total[part] += arrived(pick(at, DIRECT), part)

        away(part).start()

    for part in range(PARTS):
        away(part).wait_recv()
        out_ref[:, columns(part)] = total[part, pl.ds(pl.multiple_of(64 * x_hi, 64), 64), :] + far[part]

    for part in range(PARTS):
        away(part).wait_send()
    for index in range(len(SENDS)):
        piece(index).wait_send()

    @pl.loop(0, 8)
    def _(slot):
        for part in range(PARTS):
            twin_copy(slot, part).wait_send()

        @pl.when(owner(slot) != z)
        def _():
            for part in range(PARTS):
                for copy in z_copies(slot, part):
                    copy.wait_send()


def body(amplitudes, integrals, ij_irrep, cd_irrep):
    rows, deep = amplitudes.shape
    wide = integrals.shape[1]
    any_space = pl.BlockSpec(memory_space=pl.ANY)
    vmem = pl.BlockSpec(memory_space=pltpu.VMEM)
    dma = pltpu.SemaphoreType.DMA
    out = pl.pallas_call(
        kernel,
        out_shape=jax.ShapeDtypeStruct((64, rows), jnp.float32),
        in_specs=[any_space, any_space, vmem, vmem],
        out_specs=vmem,
        scratch_shapes=[
            pltpu.VMEM((rows, deep), jnp.bfloat16),
            pltpu.VMEM((8, deep, wide), jnp.bfloat16),
            pltpu.VMEM((8, rows, wide), jnp.float32),
            pltpu.VMEM((8, 2, 128, rows), jnp.float32),
            pltpu.VMEM((8, 128, rows), jnp.float32),
            pltpu.VMEM((8, PARTS, 128, rows // PARTS), jnp.int16),
            pltpu.VMEM((8, PARTS, 1, rows // PARTS), jnp.float32),
            pltpu.VMEM((16, PARTS, 128, rows // PARTS), jnp.int16),
            pltpu.VMEM((16, PARTS, 1, rows // PARTS), jnp.float32),
            pltpu.VMEM((PARTS, 128, rows // PARTS), jnp.float32),
            pltpu.VMEM((PARTS, 64, rows // PARTS), jnp.float32),
            pltpu.VMEM((rows, 128), jnp.bfloat16),
            dma, dma, dma((len(SENDS),)), dma((8, 4)), dma((8, PARTS)), dma((8, PARTS)),
            dma((8, PARTS)), dma((16, PARTS)), dma((8, PARTS)), dma((16, PARTS)), dma((PARTS,)), dma((PARTS,)),
        ],
        compiler_params=pltpu.CompilerParams(
            collective_id=0, has_side_effects=True, vmem_limit_bytes=60 << 20
        ),
        name="ladder",
    )(amplitudes, integrals, ij_irrep.reshape(1, rows), cd_irrep.reshape(1, deep))
    return out.T


def solution(mesh):
    in_specs = (P("occ", "vir"), P("vir", "occ"), P("occ"), P("vir"))
    out_specs = P("occ", "vir")
    return jax.shard_map(body, mesh=mesh, in_specs=in_specs, out_specs=out_specs, check_vma=False)
```
